32 devices in a mesh: grp: 4 (over y, core), dev: 8 (over z, x).
Axes of the slice: x: 2, y: 2, z: 4, core: 2. Of those that a mesh axis runs over, the one named last changes fastest.
Arguments:
- centers: bfloat16 [4096, 128], P(('grp', 'dev')), may hold values from -4 to 4
- center_weights: bfloat16 [4096, 64], P(('grp', 'dev')), may hold values from -0.75 to 0.75
- batch: bfloat16 [8192, 128], P('dev'), may hold values from -4 to 4
- labels: bfloat16 [8192, 64], P('dev'), may hold values from -6 to 6
- sub_centers: bfloat16 [2048, 128], P('grp'), may hold values from -4 to 4
- eig_vectors: bfloat16 [2048, 160], P('grp'), may hold values from -0.5 to 0.5
- eig_scale: float32 [160], replicated, may hold values from 0.02 to 0.4
Outputs:
- predictions: float32 [8192, 64], P('dev')
- center_step: float32 [4096, 64], P(('grp', 'dev'))
- nystrom_fix: float32 [2048, 64], P('grp')
The draws below stay inside these ranges and needn't reach their ends.
All inputs are finite; a program needn't handle non-finite values.
Results may differ from the reference program's by a relative error of at most 0.0031.
Values may be sent and summed in bfloat16 or wider, within the bound.
A program may use at most 64 MiB of HBM per device.

```python
import math
import jax
import jax.numpy as jnp
from jax import lax

D = 128
C = 64
QR = 160
CENTERS = 4096
BATCH = 8192
SUB = 2048


def feature_draw(key, row_total, salt):
    subkey = jax.random.fold_in(key, salt)
    column = jnp.arange(D, dtype=jnp.float32)
    spread = (column + 1.0) ** (-0.5)
    base = jax.random.truncated_normal(subkey, -4.0, 4.0, (row_total, D), jnp.float32)
    return (base * spread[None, :]).astype(jnp.bfloat16)


def draw_centers(key, part):
    return feature_draw(key, CENTERS, 101)


def draw_batch(key, part):
    return feature_draw(key, BATCH, 202)


def draw_sub_centers(key, part):
    return feature_draw(key, SUB, 303)


def levels(stream_key, dims, shards, smallest, high):
    loudness, own = 1.0, jax.random.fold_in(stream_key, 6)
    for position, parts in shards:
        heights = jnp.exp(jax.random.uniform(jax.random.fold_in(own, position), (parts,), jnp.float32, smallest / len(shards), high / len(shards)))
        loudness = loudness * jnp.repeat(heights, dims[position] // parts).reshape([-1 if axis == position else 1 for axis in range(len(dims))])
    return loudness


def scatter_about(key, shape, width, reach, shards=(), held_as=jnp.bfloat16):
    values = jax.random.normal(key, shape, jnp.float32) * width
    if len(shards) > 0:
        values = levels(key, shape, shards, -0.22, 0.18) * values
    return jnp.clip(values, min=-reach, max=reach).astype(held_as)


def setup_inputs(seed: int = 0) -> dict:
    splits = jax.random.split(jax.random.key(seed), 8)
    return {
        "centers": draw_centers(jax.random.fold_in(splits[7], 71), 0),
        "center_weights": scatter_about(splits[1], (CENTERS, C), (CENTERS // 64) ** -0.5, 0.75, ((0, 32),)),
        "batch": draw_batch(jax.random.fold_in(splits[7], 71), 0),
        "labels": scatter_about(splits[3], (BATCH, C), 1.0, 6.0, ((0, 8),)),
        "sub_centers": draw_sub_centers(jax.random.fold_in(splits[7], 71), 0),
        "eig_vectors": scatter_about(splits[5], (SUB, QR), QR ** -0.5, 0.5, ((0, 4),)),
        "eig_scale": jnp.clip(jnp.exp(jax.random.uniform(splits[6], (QR,), jnp.float32, math.log(0.02), math.log(0.4))), 0.02, 0.4),
    }


gamma_scale = 0.25
learn_rate = 8.0

def sq_norms(points):
    return lax.optimization_barrier(jnp.sum(jnp.square(points.astype(jnp.float32)), axis=1))

def kernel_tile(left, left_sq, right, right_sq):
    cross = jnp.dot(left.astype(jnp.float32), right.astype(jnp.float32).T, precision=lax.Precision.HIGHEST)
    dist = left_sq[:, None] + right_sq[None, :] - 2.0 * cross
    return jnp.exp(-gamma_scale * dist).astype(jnp.bfloat16)

def reference(centers, center_weights, batch, labels, sub_centers, eig_vectors, eig_scale):
    total = centers.shape[0]
    samples = batch.shape[0]
    width_out = center_weights.shape[1]
    block = min(1024, total)
    blocks = total // block
    batch_sq = sq_norms(batch)
    center_sq = sq_norms(centers)

    def add_block(accum, index):
        offset = (index * block).astype(jnp.int32)
        part = lax.dynamic_slice_in_dim(centers, offset, block, 0)
        part_sq = lax.dynamic_slice_in_dim(center_sq, offset, block, 0)
        part_w = lax.dynamic_slice_in_dim(center_weights, offset, block, 0)
        tile = kernel_tile(batch, batch_sq, part, part_sq)
        return (accum + jnp.dot(tile.astype(jnp.float32), part_w.astype(jnp.float32), precision=lax.Precision.HIGHEST), None)
    predictions, _ = lax.scan(add_block, jnp.zeros((samples, width_out), jnp.float32), jnp.arange(blocks, dtype=jnp.int32))
    resid = (predictions - labels.astype(jnp.float32)).astype(jnp.bfloat16)
    resid_f = resid.astype(jnp.float32)
    factor = learn_rate / math.sqrt(samples)

    def grad_block(index):
        offset = (index * block).astype(jnp.int32)
        part = lax.dynamic_slice_in_dim(centers, offset, block, 0)
        part_sq = lax.dynamic_slice_in_dim(center_sq, offset, block, 0)
        tile = kernel_tile(part, part_sq, batch, batch_sq)
        return jnp.dot(tile.astype(jnp.float32), resid_f, precision=lax.Precision.HIGHEST)
    center_step = lax.map(grad_block, jnp.arange(blocks, dtype=jnp.int32)).reshape(total, width_out) * factor
    sub_total = sub_centers.shape[0]
    sub_block = min(512, sub_total)
    sub_sq = sq_norms(sub_centers)

    def sub_grad_block(index):
        offset = (index * sub_block).astype(jnp.int32)
        part = lax.dynamic_slice_in_dim(sub_centers, offset, sub_block, 0)
        part_sq = lax.dynamic_slice_in_dim(sub_sq, offset, sub_block, 0)
        tile = kernel_tile(part, part_sq, batch, batch_sq)
        return jnp.dot(tile.astype(jnp.float32), resid_f, precision=lax.Precision.HIGHEST)
    sub_grad = lax.map(sub_grad_block, jnp.arange(sub_total // sub_block, dtype=jnp.int32)).reshape(sub_total, width_out) * factor
    vectors = eig_vectors.astype(jnp.float32)
    proj = jnp.dot(vectors.T, sub_grad, precision=lax.Precision.HIGHEST)
    nystrom_fix = jnp.dot(vectors, eig_scale.astype(jnp.float32)[:, None] * proj, precision=lax.Precision.HIGHEST)
    return (predictions, center_step, nystrom_fix)
```

```python
import functools
import math

import jax
import jax.numpy as jnp
from jax import lax
from jax.experimental import pallas as pl
from jax.experimental.pallas import tpu as pltpu
from jax.sharding import PartitionSpec as P

gamma_scale = 0.25
learn_rate = 8.0
log2e = math.log2(math.e)
MESH = pl.DeviceIdType.MESH
f32 = jnp.float32
bf16 = jnp.bfloat16

NN = (((1,), (0,)), ((), ()))
NT = (((1,), (1,)), ((), ()))
TN = (((0,), (0,)), ((), ()))


def dot(a, b, dims=NN):
    return lax.dot_general(a, b, dims, preferred_element_type=f32)


def split(x):
    hi = x.astype(bf16)
    return hi, (x - hi.astype(f32)).astype(bf16)


def kernel(
    n_dev, n_grp, factor,
    centers, weights, batch, labels, sub, eig, scale,
    pred_o, cen_o, nys_o,
    ring, w_v, batch_v, labels_v, sub_v, eig_v, scale_v,
    batch_t, batch_sq, labels_t, sub_k, tiles, resid_t,
    m_part, m_core, m_hi, pred_acc, pred_core, pred_hi, pred_t,
    grad_s, grad_r, proj_b, proj_h, pred_v, cen_v, nys_v,
    in_sem, out_sem, send_r, send_l, recv_r, recv_l,
    core_s, core_r, mhi_s, mhi_r, phi_s, phi_r, gs_s, gs_r, pb_s, pb_r,
):
    g, d = lax.axis_index("grp"), lax.axis_index("dev")
    core, hi = lax.rem(g, 2), g // 2
    n_hi = n_grp // 2
    partner = hi * 2 + (1 - core)
    half = n_dev // 2
    cb = centers.shape[0]
    width = labels.shape[1]
    rank = eig.shape[1]
    hw, hr, qr = width // 2, rank // 2, rank // 4

    odd = lax.rem(d, 2)
    pos = (1 - odd) * (d // 2) + odd * (n_dev - 1 - d // 2)

    def ring_pos(offset):
        return lax.rem(pos + (offset + n_dev), n_dev)

    def dev_at(p):
        late = p // half
        return (1 - late) * (2 * p) + late * (2 * (n_dev - p) - 1)

    right, left = dev_at(ring_pos(1)), dev_at(ring_pos(-1))
    hi_peers = [lax.rem(hi + o, n_hi) for o in range(1, n_hi)]

    barrier = pltpu.get_barrier_semaphore()
    targets = [(g, right), (g, left), (partner, d)] + [(p * 2 + core, d) for p in hi_peers]
    for target in targets:
        pl.semaphore_signal(barrier, inc=1, device_id=target, device_id_type=MESH)

    def local(src, dst, i):
        copy = pltpu.make_async_copy(src, dst, in_sem.at[i])
        copy.start()
        return copy

    c_cen = local(centers, ring.at[pos, pl.ds(0, cb)], 0)
    c_w = local(weights, w_v, 1)
    c_batch = local(batch, batch_v, 2)
    c_sub = local(sub, sub_v, 3)
    c_eig = local(eig, eig_v, 4)
    c_lab = local(labels, labels_v, 5)
    c_scale = local(scale, scale_v, 6)

    def remote(src, dst, ssem, rsem, target):
        copy = pltpu.make_async_remote_copy(
            src_ref=src, dst_ref=dst, send_sem=ssem, recv_sem=rsem,
            device_id=target, device_id_type=MESH,
        )
        copy.start()
        return copy

    c_w.wait()
    ring[pos, cb:, :] = w_v[...].astype(f32).T.astype(bf16)
    c_cen.wait()
    pl.semaphore_wait(barrier, len(targets))

    rows = cb + width
    cut = rows // 2
    halves = (pl.ds(0, cut), pl.ds(cut, rows - cut))
    sent = []

    def parts(step, way):
        return (0, 1) if step < half else ((0,) if way > 0 else (1,))

    def send(step, way, part):
        block = ring.at[ring_pos(-way * (step - 1)), halves[part]]
        ss, rs = (send_r, recv_r) if way > 0 else (send_l, recv_l)
        sent.append(remote(block, block, ss.at[step - 1, part], rs.at[step - 1, part],
                           (g, right if way > 0 else left)))

    def arrive(step, way, part):
        block = ring.at[ring_pos(-way * step), halves[part]]
        ss, rs = (send_r, recv_r) if way > 0 else (send_l, recv_l)
        pltpu.make_async_remote_copy(
            src_ref=block, dst_ref=block, send_sem=ss.at[step - 1, part],
            recv_sem=rs.at[step - 1, part],
            device_id=(g, right if way > 0 else left), device_id_type=MESH,
        ).wait_recv()

    def pass_on(step):
        for part in (0, 1):
            for way in (1, -1):
                if part in parts(step, way):
                    arrive(step, way, part)
                    if step < half and part in parts(step + 1, way):
                        send(step + 1, way, part)

    for part in (0, 1):
        for way in (1, -1):
            if part in parts(1, way):
                send(1, way, part)

    a2 = gamma_scale * log2e
    c_batch.wait()
    b_t = batch_v[...].astype(f32).T
    batch_t[...] = b_t.astype(bf16)
    batch_sq[...] = jnp.sum(b_t * b_t, axis=0, keepdims=True) * a2

    def tile(points):
        cross = dot(points, batch_t[...])
        p32 = points.astype(f32)
        sq = jnp.sum(p32 * p32, axis=1, keepdims=True) * a2
        return jnp.exp2(cross * (2.0 * a2) - (sq + batch_sq[...])).astype(bf16)

    def center_tile(p, first=False):
        t = tile(ring[p, :cb, :])
        tiles[p] = t
        add = dot(ring[p, cb:, :], t)
        pred_acc[...] = add if first else pred_acc[...] + add

    c_sub.wait()
    s_rows = sub_v.shape[0]
    s_block = min(cb, s_rows)
    s_blocks = s_rows // s_block

    def sub_tiles(low, high):
        for i in range(low, high):
            block = slice(i * s_block, (i + 1) * s_block)
            sub_k[block, :] = tile(sub_v[block, :])

    sub_tiles(0, s_blocks // 2)
    pass_on(1)
    sub_tiles(s_blocks // 2, s_blocks)
    c_eig.wait()
    m_part[...] = dot(eig_v[...], sub_k[...], TN)
    theirs = pl.ds(pl.multiple_of((1 - core) * hr, 8), hr)
    mine = pl.ds(pl.multiple_of(core * hr, 8), hr)
    m_send = remote(m_part.at[theirs], m_core, core_s.at[0], core_r.at[0], (partner, d))
    center_tile(pos, True)
    c_lab.wait()
    c_scale.wait()
    labels_t[...] = labels_v[...].astype(f32).T

    m_sends, waited = [], False
    for step in range(2, half + 1):
        pass_on(step)
        center_tile(ring_pos(-(step - 1)))
        center_tile(ring_pos(step - 1))
        if step == 2:
            m_send.wait()
            m_hi[hi] = (m_part[mine, :] + m_core[...]).astype(bf16)
            for o in range(1, n_hi):
                m_sends.append(remote(m_hi.at[hi], m_hi.at[hi], mhi_s.at[o - 1], mhi_r.at[o - 1],
                                      (hi_peers[o - 1] * 2 + core, d)))
    center_tile(ring_pos(half))

    theirs_w = pl.ds(pl.multiple_of((1 - core) * hw, 8), hw)
    mine_w = pl.ds(pl.multiple_of(core * hw, 8), hw)
    p_send = remote(pred_acc.at[theirs_w], pred_core, core_s.at[1], core_r.at[1], (partner, d))

    for c in m_sends:
        c.wait()
    m_sum = m_hi[0].astype(f32)
    for i in range(1, n_hi):
        m_sum = m_sum + m_hi[i].astype(f32)
    mh, ml = split(m_sum * factor)

    p_send.wait()
    pred_hi[hi] = pred_acc[mine_w, :] + pred_core[...]
    p_sends = []
    for o in range(1, n_hi):
        p_sends.append(remote(pred_hi.at[hi], pred_hi.at[hi], phi_s.at[o - 1], phi_r.at[o - 1],
                              (hi_peers[o - 1] * 2 + core, d)))
    for c in p_sends:
        c.wait()
    total = pred_hi[0]
    for i in range(1, n_hi):
        total = total + pred_hi[i]
    pred_t[core] = total
    f_send = remote(pred_t.at[core], pred_t.at[core], core_s.at[2], core_r.at[2], (partner, d))
    f_send.wait()

    pred = jnp.concatenate([pred_t[0], pred_t[1]], axis=0)
    resid_t[...] = (pred - labels_t[...]).astype(bf16)
    r_t = resid_t[...]
    proj = dot(mh, r_t, NT) + dot(ml, r_t, NT)
    proj_b[d] = jnp.concatenate([proj[:qr], proj[qr:]], axis=1)
    away = []
    for k in range(half):
        away += [half] if k == 0 else [half - k, k - half]
    pb = []
    for j, o in enumerate(away):
        pb.append(remote(proj_b.at[d], proj_b.at[d], pb_s.at[j], pb_r.at[j], (g, dev_at(ring_pos(o)))))
    gs = []
    for j, o in enumerate(away):
        q = ring_pos(o)
        grad_s[j] = dot(r_t, tiles[q], NT).astype(bf16)
        gs.append(remote(grad_s.at[j], grad_r.at[j], gs_s.at[j], gs_r.at[j], (g, dev_at(q))))
    grad = dot(r_t, tiles[pos], NT)

    pred_v[...] = pred.T
    o_pred = pltpu.make_async_copy(pred_v, pred_o, out_sem.at[0])
    o_pred.start()

    sc = scale_v[...]
    r_i = lax.broadcasted_iota(jnp.int32, (rank, rank), 0)
    c_i = lax.broadcasted_iota(jnp.int32, (rank, rank), 1)
    sc_col = jnp.sum(jnp.where(r_i == c_i, sc, 0.0), axis=1, keepdims=True)

    for c in pb:
        c.wait()
    p_sum = proj_b[0]
    for i in range(1, n_dev):
        p_sum = p_sum + proj_b[i]
    proj_h[core] = p_sum
    h_send = remote(proj_h.at[core], proj_h.at[core], core_s.at[3], core_r.at[3], (partner, d))

    for c in gs:
        c.wait()
    for j in range(n_dev - 1):
        grad = grad + grad_r[j].astype(f32)
    cen_v[...] = (grad * factor).T
    o_cen = pltpu.make_async_copy(cen_v, cen_o, out_sem.at[1])
    o_cen.start()

    h_send.wait()
    top, low = proj_h[0], proj_h[1]
    full = jnp.concatenate([top[:, :width], top[:, width:], low[:, :width], low[:, width:]], axis=0)
    fh, fl = split(full * sc_col)
    nys_v[...] = dot(eig_v[...], fh) + dot(eig_v[...], fl)
    o_nys = pltpu.make_async_copy(nys_v, nys_o, out_sem.at[2])
    o_nys.start()
    for c in sent:
        c.wait_send()
    o_pred.wait()
    o_cen.wait()
    o_nys.wait()


def body(n_dev, n_grp, centers, center_weights, batch, labels, sub_centers, eig_vectors, eig_scale):
    cb, width_in = centers.shape
    width = center_weights.shape[1]
    samples = batch.shape[0]
    s_rows, rank = eig_vectors.shape
    n_hi, half = n_grp // 2, n_dev // 2
    others, peers = n_dev - 1, max(n_hi - 1, 1)
    hw, hr, qr = width // 2, rank // 2, rank // 4
    factor = learn_rate / math.sqrt(samples * n_dev)
    V, dma = pltpu.VMEM, pltpu.SemaphoreType.DMA
    any_spec = pl.BlockSpec(memory_space=pl.ANY)
    return pl.pallas_call(
        functools.partial(kernel, n_dev, n_grp, factor),
        out_shape=(
            jax.ShapeDtypeStruct((samples, width), f32),
            jax.ShapeDtypeStruct((cb, width), f32),
            jax.ShapeDtypeStruct((s_rows, width), f32),
        ),
        in_specs=[any_spec] * 7,
        out_specs=(any_spec,) * 3,
        scratch_shapes=[
            V((n_dev, cb + width, width_in), bf16),
            V((cb, width), bf16),
            V((samples, width_in), bf16),
            V((samples, width), bf16),
            V((s_rows, width_in), bf16),
            V((s_rows, rank), bf16),
            V((1, rank), f32),
            V((width_in, samples), bf16),
            V((1, samples), f32),
            V((width, samples), f32),
            V((s_rows, samples), bf16),
            V((n_dev, cb, samples), bf16),
            V((width, samples), bf16),
            V((rank, samples), f32),
            V((hr, samples), f32),
            V((n_hi, hr, samples), bf16),
            V((width, samples), f32),
            V((hw, samples), f32),
            V((n_hi, hw, samples), f32),
            V((2, hw, samples), f32),
            V((others, width, cb), bf16),
            V((others, width, cb), bf16),
            V((n_dev, qr, 2 * width), f32),
            V((2, qr, 2 * width), f32),
            V((samples, width), f32),
            V((cb, width), f32),
            V((s_rows, width), f32),
            dma((7,)), dma((3,)),
            dma((half, 2)), dma((half, 2)), dma((half, 2)), dma((half, 2)),
            dma((4,)), dma((4,)),
            dma((peers,)), dma((peers,)), dma((peers,)), dma((peers,)),
            dma((others,)), dma((others,)), dma((others,)), dma((others,)),
        ],
        compiler_params=pltpu.CompilerParams(
            collective_id=0, has_side_effects=True, vmem_limit_bytes=60000 * 1024
        ),
        name="eigenpro_step",
    )(centers, center_weights, batch, labels, sub_centers, eig_vectors, eig_scale.reshape(1, -1))


def solution(mesh):
    placed = (
        P(("grp", "dev"), None),
        P(("grp", "dev"), None),
        P("dev", None),
        P("dev", None),
        P("grp", None),
        P("grp", None),
        P(),
    )
    return jax.shard_map(
        functools.partial(body, mesh.shape["dev"], mesh.shape["grp"]),
        mesh=mesh,
        in_specs=placed,
        out_specs=(P("dev", None), P(("grp", "dev"), None), P("grp", None)),
        check_vma=False,
    )
```

```python
import functools
import math

import jax
import jax.numpy as jnp
from jax import lax
from jax.experimental import pallas as pl
from jax.experimental.pallas import tpu as pltpu
from jax.sharding import PartitionSpec as P

gamma_scale = 0.25
learn_rate = 8.0
log2e = math.log2(math.e)
MESH = pl.DeviceIdType.MESH
f32 = jnp.float32
bf16 = jnp.bfloat16

NN = (((1,), (0,)), ((), ()))
NT = (((1,), (1,)), ((), ()))
TN = (((0,), (0,)), ((), ()))


def dot(a, b, dims=NN):
    return lax.dot_general(a, b, dims, preferred_element_type=f32)


def split(x):
    hi = x.astype(bf16)
    return hi, (x - hi.astype(f32)).astype(bf16)


def kernel(
    n_dev, n_grp, factor,
    centers, weights, batch, labels, sub, eig, scale,
    pred_o, cen_o, nys_o,
    ring, batch_v, labels_v, sub_v, eig_v, scale_v,
    batch_t, batch_sq, sub_k, tiles, resid_t,
    m_part, m_core, m_hi, pred_acc, pred_core, pred_hi, pred_t,
    grad_s, grad_r, proj_b, proj_h, cen_v, nys_v,
    in_sem, out_sem, send_r, send_l, recv_r, recv_l,
    core_s, core_r, mhi_s, mhi_r, phi_s, phi_r, gs_s, gs_r, pb_s, pb_r,
):
    g, d = lax.axis_index("grp"), lax.axis_index("dev")
    core, hi = lax.rem(g, 2), g // 2
    n_hi = n_grp // 2
    partner = hi * 2 + (1 - core)
    half = n_dev // 2
    cb = centers.shape[0]
    width = labels.shape[0]
    rank = eig.shape[0]
    hw, hr, qr = width // 2, rank // 2, rank // 4

    odd = lax.rem(d, 2)
    pos = (1 - odd) * (d // 2) + odd * (n_dev - 1 - d // 2)

    def ring_pos(offset):
        return lax.rem(pos + (offset + n_dev), n_dev)

    def dev_at(p):
        late = p // half
        return (1 - late) * (2 * p) + late * (2 * (n_dev - p) - 1)

    right, left = dev_at(ring_pos(1)), dev_at(ring_pos(-1))
    hi_peers = [lax.rem(hi + o, n_hi) for o in range(1, n_hi)]

    barrier = pltpu.get_barrier_semaphore()
    targets = [(g, right), (g, left), (partner, d)] + [(p * 2 + core, d) for p in hi_peers]
    for target in targets:
        pl.semaphore_signal(barrier, inc=1, device_id=target, device_id_type=MESH)

    def local(src, dst, i):
        copy = pltpu.make_async_copy(src, dst, in_sem.at[i])
        copy.start()
        return copy

    c_cen = local(centers, ring.at[pos, pl.ds(0, cb)], 0)
    c_w = local(weights, ring.at[pos, pl.ds(cb, width)], 1)
    c_batch = local(batch, batch_v, 2)
    c_sub = local(sub, sub_v, 3)
    c_eig = local(eig, eig_v, 4)
    c_lab = local(labels, labels_v, 5)
    c_scale = local(scale, scale_v, 6)

    def remote(src, dst, ssem, rsem, target):
        copy = pltpu.make_async_remote_copy(
            src_ref=src, dst_ref=dst, send_sem=ssem, recv_sem=rsem,
            device_id=target, device_id_type=MESH,
        )
        copy.start()
        return copy

    c_w.wait()
    c_cen.wait()
    pl.semaphore_wait(barrier, len(targets))

    rows = cb + width
    cut = rows // 2
    halves = (pl.ds(0, cut), pl.ds(cut, rows - cut))
    sent = []

    def parts(step, way):
        return (0, 1) if step < half else ((0,) if way > 0 else (1,))

    def send(step, way, part):
        block = ring.at[ring_pos(-way * (step - 1)), halves[part]]
        ss, rs = (send_r, recv_r) if way > 0 else (send_l, recv_l)
        sent.append(remote(block, block, ss.at[step - 1, part], rs.at[step - 1, part],
                           (g, right if way > 0 else left)))

    def arrive(step, way, part):
        block = ring.at[ring_pos(-way * step), halves[part]]
        ss, rs = (send_r, recv_r) if way > 0 else (send_l, recv_l)
        pltpu.make_async_remote_copy(
            src_ref=block, dst_ref=block, send_sem=ss.at[step - 1, part],
            recv_sem=rs.at[step - 1, part],
            device_id=(g, right if way > 0 else left), device_id_type=MESH,
        ).wait_recv()

    def pass_on(step):
        for part in (0, 1):
            for way in (1, -1):
                if part in parts(step, way):
                    arrive(step, way, part)
                    if step < half and part in parts(step + 1, way):
                        send(step + 1, way, part)

    for part in (0, 1):
        for way in (1, -1):
            if part in parts(1, way):
                send(1, way, part)

    a2 = gamma_scale * log2e
    c_batch.wait()
    b_t = batch_v[...].astype(f32).T
    batch_t[...] = b_t.astype(bf16)
    batch_sq[...] = jnp.sum(b_t * b_t, axis=0, keepdims=True) * a2

    def tile(points):
        cross = dot(points, batch_t[...])
        p32 = points.astype(f32)
        sq = jnp.sum(p32 * p32, axis=1, keepdims=True) * a2
        return jnp.exp2(cross * (2.0 * a2) - (sq + batch_sq[...])).astype(bf16)

    def center_tile(p, first=False):
        t = tile(ring[p, :cb, :])
        tiles[p] = t
        add = dot(ring[p, cb:, :], t)
        pred_acc[...] = add if first else pred_acc[...] + add

    c_sub.wait()
    s_rows = sub_v.shape[0]
    s_block = min(cb, s_rows)
    s_blocks = s_rows // s_block

    def sub_tiles(low, high):
        for i in range(low, high):
            block = slice(i * s_block, (i + 1) * s_block)
            sub_k[block, :] = tile(sub_v[block, :])

    sub_tiles(0, s_blocks // 2)
    pass_on(1)
    sub_tiles(s_blocks // 2, s_blocks)
    c_eig.wait()
    m_part[...] = dot(eig_v[...], sub_k[...])
    theirs = pl.ds(pl.multiple_of((1 - core) * hr, 8), hr)
    mine = pl.ds(pl.multiple_of(core * hr, 8), hr)
    m_send = remote(m_part.at[theirs], m_core, core_s.at[0], core_r.at[0], (partner, d))
    center_tile(pos, True)
    c_lab.wait()
    c_scale.wait()

    m_sends, waited = [], False
    for step in range(2, half + 1):
        pass_on(step)
        center_tile(ring_pos(-(step - 1)))
        center_tile(ring_pos(step - 1))
        if step == 2:
            m_send.wait()
            m_hi[hi] = (m_part[mine, :] + m_core[...]).astype(bf16)
            for o in range(1, n_hi):
                m_sends.append(remote(m_hi.at[hi], m_hi.at[hi], mhi_s.at[o - 1], mhi_r.at[o - 1],
                                      (hi_peers[o - 1] * 2 + core, d)))
    center_tile(ring_pos(half))

    theirs_w = pl.ds(pl.multiple_of((1 - core) * hw, 8), hw)
    mine_w = pl.ds(pl.multiple_of(core * hw, 8), hw)
    p_send = remote(pred_acc.at[theirs_w], pred_core, core_s.at[1], core_r.at[1], (partner, d))

    for c in m_sends:
        c.wait()
    m_sum = m_hi[0].astype(f32)
    for i in range(1, n_hi):
        m_sum = m_sum + m_hi[i].astype(f32)
    mh, ml = split(m_sum * factor)

    p_send.wait()
    pred_hi[hi] = pred_acc[mine_w, :] + pred_core[...]
    p_sends = []
    for o in range(1, n_hi):
        p_sends.append(remote(pred_hi.at[hi], pred_hi.at[hi], phi_s.at[o - 1], phi_r.at[o - 1],
                              (hi_peers[o - 1] * 2 + core, d)))
    for c in p_sends:
        c.wait()
    total = pred_hi[0]
    for i in range(1, n_hi):
        total = total + pred_hi[i]
    pred_t[core] = total
    f_send = remote(pred_t.at[core], pred_t.at[core], core_s.at[2], core_r.at[2], (partner, d))
    f_send.wait()

    pred = pred_t[...].reshape(width, pred_t.shape[2])
    o_pred = [
        pltpu.make_async_copy(pred_t.at[i], pred_o.at[pl.ds(i * hw, hw)], out_sem.at[2 + i])
        for i in range(2)
    ]
    for c in o_pred:
        c.start()
    resid_t[...] = (pred - labels_v[...].astype(f32)).astype(bf16)
    r_t = resid_t[...]
    proj = dot(mh, r_t, NT) + dot(ml, r_t, NT)
    proj_b[d] = jnp.concatenate([proj[:qr], proj[qr:]], axis=1)
    away = []
    for k in range(half):
        away += [half] if k == 0 else [half - k, k - half]
    pb = []
    for j, o in enumerate(away):
        pb.append(remote(proj_b.at[d], proj_b.at[d], pb_s.at[j], pb_r.at[j], (g, dev_at(ring_pos(o)))))
    gs = []
    for j, o in enumerate(away):
        q = ring_pos(o)
        grad_s[j] = dot(r_t, tiles[q], NT).astype(bf16)
        gs.append(remote(grad_s.at[j], grad_r.at[j], gs_s.at[j], gs_r.at[j], (g, dev_at(q))))
    grad = dot(r_t, tiles[pos], NT)

    sc = scale_v[...]
    r_i = lax.broadcasted_iota(jnp.int32, (rank, rank), 0)
    c_i = lax.broadcasted_iota(jnp.int32, (rank, rank), 1)
    sc_col = jnp.sum(jnp.where(r_i == c_i, sc, 0.0), axis=1, keepdims=True)

    for c in pb:
        c.wait()
    p_sum = proj_b[0]
    for i in range(1, n_dev):
        p_sum = p_sum + proj_b[i]
    proj_h[core] = p_sum
    h_send = remote(proj_h.at[core], proj_h.at[core], core_s.at[3], core_r.at[3], (partner, d))

    for c in gs:
        c.wait()
    for j in range(n_dev - 1):
        grad = grad + grad_r[j].astype(f32)
    cen_v[...] = grad * factor
    o_cen = pltpu.make_async_copy(cen_v, cen_o, out_sem.at[0])
    o_cen.start()

    h_send.wait()
    top, low = proj_h[0], proj_h[1]
    full = jnp.concatenate([top[:, :width], top[:, width:], low[:, :width], low[:, width:]], axis=0)
    fh, fl = split(full * sc_col)
    nys_v[...] = dot(fh, eig_v[...], TN) + dot(fl, eig_v[...], TN)
    o_nys = pltpu.make_async_copy(nys_v, nys_o, out_sem.at[1])
    o_nys.start()
    for c in sent:
        c.wait_send()
    for c in o_pred:
        c.wait()
    o_cen.wait()
    o_nys.wait()


def body(n_dev, n_grp, centers, center_weights, batch, labels, sub_centers, eig_vectors, eig_scale):
    cb, width_in = centers.shape
    width = center_weights.shape[1]
    samples = batch.shape[0]
    s_rows, rank = eig_vectors.shape
    n_hi, half = n_grp // 2, n_dev // 2
    others, peers = n_dev - 1, max(n_hi - 1, 1)
    hw, hr, qr = width // 2, rank // 2, rank // 4
    factor = learn_rate / math.sqrt(samples * n_dev)
    V, dma = pltpu.VMEM, pltpu.SemaphoreType.DMA
    any_spec = pl.BlockSpec(memory_space=pl.ANY)
    outs = pl.pallas_call(
        functools.partial(kernel, n_dev, n_grp, factor),
        out_shape=(
            jax.ShapeDtypeStruct((width, samples), f32),
            jax.ShapeDtypeStruct((width, cb), f32),
            jax.ShapeDtypeStruct((width, s_rows), f32),
        ),
        in_specs=[any_spec] * 7,
        out_specs=(any_spec,) * 3,
        scratch_shapes=[
            V((n_dev, cb + width, width_in), bf16),
            V((samples, width_in), bf16),
            V((width, samples), bf16),
            V((s_rows, width_in), bf16),
            V((rank, s_rows), bf16),
            V((1, rank), f32),
            V((width_in, samples), bf16),
            V((1, samples), f32),
            V((s_rows, samples), bf16),
            V((n_dev, cb, samples), bf16),
            V((width, samples), bf16),
            V((rank, samples), f32),
            V((hr, samples), f32),
            V((n_hi, hr, samples), bf16),
            V((width, samples), f32),
            V((hw, samples), f32),
            V((n_hi, hw, samples), f32),
            V((2, hw, samples), f32),
            V((others, width, cb), bf16),
            V((others, width, cb), bf16),
            V((n_dev, qr, 2 * width), f32),
            V((2, qr, 2 * width), f32),
            V((width, cb), f32),
            V((width, s_rows), f32),
            dma((7,)), dma((4,)),
            dma((half, 2)), dma((half, 2)), dma((half, 2)), dma((half, 2)),
            dma((4,)), dma((4,)),
            dma((peers,)), dma((peers,)), dma((peers,)), dma((peers,)),
            dma((others,)), dma((others,)), dma((others,)), dma((others,)),
        ],
        compiler_params=pltpu.CompilerParams(
            collective_id=0, has_side_effects=True, vmem_limit_bytes=60000 * 1024
        ),
        name="eigenpro_step",
    )(centers, center_weights.T, batch, labels.T, sub_centers, eig_vectors.T, eig_scale.reshape(1, -1))
    return tuple(out.T for out in outs)


def solution(mesh):
    placed = (
        P(("grp", "dev"), None),
        P(("grp", "dev"), None),
        P("dev", None),
        P("dev", None),
        P("grp", None),
        P("grp", None),
        P(),
    )
    return jax.shard_map(
        functools.partial(body, mesh.shape["dev"], mesh.shape["grp"]),
        mesh=mesh,
        in_specs=placed,
        out_specs=(P("dev", None), P(("grp", "dev"), None), P("grp", None)),
        check_vma=False,
    )
```

```python
import functools
import math

import jax
import jax.numpy as jnp
from jax import lax
from jax.experimental import pallas as pl
from jax.experimental.pallas import tpu as pltpu
from jax.sharding import PartitionSpec as P

gamma_scale = 0.25
learn_rate = 8.0
log2e = math.log2(math.e)
MESH = pl.DeviceIdType.MESH
f32 = jnp.float32
bf16 = jnp.bfloat16

ring_parts = 4
pred_parts = 4

NN = (((1,), (0,)), ((), ()))
NT = (((1,), (1,)), ((), ()))
TN = (((0,), (0,)), ((), ()))


def dot(a, b, dims=NN):
    return lax.dot_general(a, b, dims, preferred_element_type=f32)


def split(x):
    hi = x.astype(bf16)
    return hi, (x - hi.astype(f32)).astype(bf16)


def kernel(
    n_dev, n_grp, factor,
    centers, weights, batch, labels, sub, eig, scale,
    pred_o, cen_o, nys_o,
    ring, batch_v, labels_v, sub_v, eig_v, scale_v,
    batch_t, batch_sq, sub_k, tiles, resid,
    m_part, m_core, m_hi, pred_acc, pred_core, pred_hi, pred_t,
    grad_s, grad_r, proj_b, proj_h, cen_v, nys_v,
    in_sem, out_sem, send_r, send_l, recv_r, recv_l,
    core_s, core_r, pc_s, pc_r, pf_s, pf_r, mhi_s, mhi_r, phi_s, phi_r, gs_s, gs_r, pb_s, pb_r,
):
    g, d = lax.axis_index("grp"), lax.axis_index("dev")
    core, hi = lax.rem(g, 2), g // 2
    n_hi = n_grp // 2
    partner = hi * 2 + (1 - core)
    half = n_dev // 2
    cb = centers.shape[0]
    width = labels.shape[0]
    rank = eig.shape[0]
    hw, hr, qr = width // 2, rank // 2, rank // 4

    odd = lax.rem(d, 2)
    pos = (1 - odd) * (d // 2) + odd * (n_dev - 1 - d // 2)

    def ring_pos(offset):
        return lax.rem(pos + (offset + n_dev), n_dev)

    def dev_at(p):
        late = p // half
        return (1 - late) * (2 * p) + late * (2 * (n_dev - p) - 1)

    right, left = dev_at(ring_pos(1)), dev_at(ring_pos(-1))
    hi_peers = [lax.rem(hi + o, n_hi) for o in range(1, n_hi)]

    barrier = pltpu.get_barrier_semaphore()
    targets = [(g, right), (g, left), (partner, d)] + [(p * 2 + core, d) for p in hi_peers]
    for target in targets:
        pl.semaphore_signal(barrier, inc=1, device_id=target, device_id_type=MESH)

    def local(src, dst, i):
        copy = pltpu.make_async_copy(src, dst, in_sem.at[i])
        copy.start()
        return copy

    c_cen = local(centers, ring.at[pos, pl.ds(0, cb)], 0)
    c_w = local(weights, ring.at[pos, pl.ds(cb, width)], 1)
    c_batch = local(batch, batch_v, 2)
    c_sub = local(sub, sub_v, 3)
    c_eig = local(eig, eig_v, 4)
    c_lab = local(labels, labels_v, 5)
    c_scale = local(scale, scale_v, 6)

    def remote(src, dst, ssem, rsem, target):
        copy = pltpu.make_async_remote_copy(
            src_ref=src, dst_ref=dst, send_sem=ssem, recv_sem=rsem,
            device_id=target, device_id_type=MESH,
        )
        copy.start()
        return copy

    c_w.wait()
    c_cen.wait()
    pl.semaphore_wait(barrier, len(targets))

    rows = cb + width
    cut = rows // ring_parts
    pieces = [pl.ds(i * cut, cut) for i in range(ring_parts)]
    sent = []

    def parts(step, way):
        every = tuple(range(ring_parts))
        middle = ring_parts // 2
        return every if step < half else (every[:middle] if way > 0 else every[middle:])

    def send(step, way, part):
        block = ring.at[ring_pos(-way * (step - 1)), pieces[part]]
        ss, rs = (send_r, recv_r) if way > 0 else (send_l, recv_l)
        sent.append(remote(block, block, ss.at[step - 1, part], rs.at[step - 1, part],
                           (g, right if way > 0 else left)))

    def arrive(step, way, part):
        block = ring.at[ring_pos(-way * step), pieces[part]]
        ss, rs = (send_r, recv_r) if way > 0 else (send_l, recv_l)
        pltpu.make_async_remote_copy(
            src_ref=block, dst_ref=block, send_sem=ss.at[step - 1, part],
            recv_sem=rs.at[step - 1, part],
            device_id=(g, right if way > 0 else left), device_id_type=MESH,
        ).wait_recv()

    def pass_on(step):
        for part in range(ring_parts):
            for way in (1, -1):
                if part in parts(step, way):
                    arrive(step, way, part)
                    if step < half and part in parts(step + 1, way):
                        send(step + 1, way, part)

    for part in range(ring_parts):
        for way in (1, -1):
            if part in parts(1, way):
                send(1, way, part)

    a2 = gamma_scale * log2e
    c_batch.wait()
    b_t = batch_v[...].astype(f32).T
    batch_t[...] = b_t.astype(bf16)
    batch_sq[...] = jnp.sum(b_t * b_t, axis=0, keepdims=True) * a2

    def tile(points):
        cross = dot(points, batch_t[...])
        p32 = points.astype(f32)
        sq = jnp.sum(p32 * p32, axis=1, keepdims=True) * a2
        return jnp.exp2(cross * (2.0 * a2) - (sq + batch_sq[...])).astype(bf16)

    away = [half]
    for k in range(1, half):
        away += [half - k, k - half]
    slots = away + [0]

    def center_tile(offset, first=False):
        p = ring_pos(offset)
        t = tile(ring[p, :cb, :])
        tiles[slots.index(offset)] = t
        add = dot(ring[p, cb:, :], t)
        pred_acc[...] = add if first else pred_acc[...] + add

    c_sub.wait()
    s_rows = sub_v.shape[0]
    s_block = min(cb, s_rows)
    s_blocks = s_rows // s_block

    def sub_tiles(low, high):
        for i in range(low, high):
            block = slice(i * s_block, (i + 1) * s_block)
            sub_k[block, :] = tile(sub_v[block, :])

    sub_tiles(0, s_blocks)
    c_eig.wait()
    m_part[...] = dot(eig_v[...], sub_k[...])
    theirs = pl.ds(pl.multiple_of((1 - core) * hr, 8), hr)
    mine = pl.ds(pl.multiple_of(core * hr, 8), hr)
    m_send = remote(m_part.at[theirs], m_core, core_s.at[0], core_r.at[0], (partner, d))
    center_tile(0, True)
    c_lab.wait()
    c_scale.wait()

    m_sends = []
    for step in range(1, half):
        pass_on(step)
        center_tile(-step)
        center_tile(step)
        if step == min(2, half - 1):
            m_send.wait()
            m_hi[hi] = (m_part[mine, :] + m_core[...]).astype(bf16)
            for o in range(1, n_hi):
                m_sends.append(remote(m_hi.at[hi], m_hi.at[hi], mhi_s.at[o - 1], mhi_r.at[o - 1],
                                      (hi_peers[o - 1] * 2 + core, d)))
    pass_on(half)
    center_tile(half)

    theirs_w = pl.ds(pl.multiple_of((1 - core) * hw, 8), hw)
    mine_w = pl.ds(pl.multiple_of(core * hw, 8), hw)
    n_cols = pred_acc.shape[1] // pred_parts
    cols = [pl.ds(k * n_cols, n_cols) for k in range(pred_parts)]
    p_send = [
        remote(pred_acc.at[theirs_w, cols[k]], pred_core.at[:, cols[k]],
               pc_s.at[k], pc_r.at[k], (partner, d))
        for k in range(pred_parts)
    ]

    for c in m_sends:
        c.wait()
    m_sum = m_hi[0].astype(f32)
    for i in range(1, n_hi):
        m_sum = m_sum + m_hi[i].astype(f32)
    mh, ml = split(m_sum * factor)

    p_sends = []
    for k in range(pred_parts):
        p_send[k].wait()
        pred_hi[k, hi] = (pred_acc[mine_w, cols[k]] + pred_core[:, cols[k]]).astype(bf16)
        p_sends.append([
            remote(pred_hi.at[k, hi], pred_hi.at[k, hi], phi_s.at[k, o - 1], phi_r.at[k, o - 1],
                   (hi_peers[o - 1] * 2 + core, d))
            for o in range(1, n_hi)
        ])
    f_send = []
    for k in range(pred_parts):
        for c in p_sends[k]:
            c.wait()
        total = pred_hi[k, 0].astype(f32)
        for i in range(1, n_hi):
            total = total + pred_hi[k, i].astype(f32)
        pred_t[mine_w, cols[k]] = total
        place = pred_t.at[mine_w, cols[k]]
        f_send.append(remote(place, place, pf_s.at[k], pf_r.at[k], (partner, d)))
    for k in range(pred_parts):
        f_send[k].wait()
        resid[cols[k], :] = (pred_t[:, cols[k]] - labels_v[:, cols[k]].astype(f32)).T.astype(bf16)

    r = resid[...]
    proj = dot(mh, r) + dot(ml, r)
    proj_b[d] = jnp.concatenate([proj[:qr], proj[qr:]], axis=1).astype(bf16)
    pb = []
    for j, o in enumerate(away):
        pb.append(remote(proj_b.at[d], proj_b.at[d], pb_s.at[j], pb_r.at[j], (g, dev_at(ring_pos(o)))))
    o_pred = pltpu.make_async_copy(pred_t, pred_o, out_sem.at[2])
    o_pred.start()
    gs = []
    group = min(4, n_dev)
    for low in range(0, n_dev, group):
        stack = tiles[low:low + group].reshape(group * cb, tiles.shape[2])
        grads = dot(stack, r)
        for j in range(low, low + group):
            part = grads[(j - low) * cb:(j - low + 1) * cb].T
            if j == n_dev - 1:
                grad = part
            else:
                grad_s[j] = part.astype(bf16)
                gs.append(remote(grad_s.at[j], grad_r.at[j], gs_s.at[j], gs_r.at[j],
                                 (g, dev_at(ring_pos(away[j])))))

    sc = scale_v[...]
    r_i = lax.broadcasted_iota(jnp.int32, (rank, rank), 0)
    c_i = lax.broadcasted_iota(jnp.int32, (rank, rank), 1)
    sc_col = jnp.sum(jnp.where(r_i == c_i, sc, 0.0), axis=1, keepdims=True)

    for c in pb:
        c.wait()
    p_sum = proj_b[0].astype(f32)
    for i in range(1, n_dev):
        p_sum = p_sum + proj_b[i].astype(f32)
    proj_h[core] = p_sum
    h_send = remote(proj_h.at[core], proj_h.at[core], core_s.at[3], core_r.at[3], (partner, d))

    for c in gs:
        c.wait()
    for j in range(n_dev - 1):
        grad = grad + grad_r[j].astype(f32)
    cen_v[...] = grad * factor
    o_cen = pltpu.make_async_copy(cen_v, cen_o, out_sem.at[0])
    o_cen.start()

    h_send.wait()
    top, low = proj_h[0], proj_h[1]
    full = jnp.concatenate([top[:, :width], top[:, width:], low[:, :width], low[:, width:]], axis=0)
    fh, fl = split(full * sc_col)
    nys_v[...] = dot(fh, eig_v[...], TN) + dot(fl, eig_v[...], TN)
    o_nys = pltpu.make_async_copy(nys_v, nys_o, out_sem.at[1])
    o_nys.start()
    for c in sent:
        c.wait_send()
    o_pred.wait()
    o_cen.wait()
    o_nys.wait()


def place(*refs):
    ins, outs, sem = refs[:3], refs[3:6], refs[6]
    copies = [pltpu.make_async_copy(a, b, sem.at[i]) for i, (a, b) in enumerate(zip(ins, outs))]
    for c in copies:
        c.start()
    for c in copies:
        c.wait()


def body(n_dev, n_grp, centers, center_weights, batch, labels, sub_centers, eig_vectors, eig_scale):
    cb, width_in = centers.shape
    width = center_weights.shape[1]
    samples = batch.shape[0]
    s_rows, rank = eig_vectors.shape
    n_hi, half = n_grp // 2, n_dev // 2
    others, peers = n_dev - 1, max(n_hi - 1, 1)
    hw, hr, qr = width // 2, rank // 2, rank // 4
    factor = learn_rate / math.sqrt(samples * n_dev)
    V, dma = pltpu.VMEM, pltpu.SemaphoreType.DMA
    any_spec = pl.BlockSpec(memory_space=pl.ANY)
    outs = pl.pallas_call(
        functools.partial(kernel, n_dev, n_grp, factor),
        out_shape=(
            pltpu.VMEM((width, samples), f32),
            pltpu.VMEM((width, cb), f32),
            pltpu.VMEM((width, s_rows), f32),
        ),
        in_specs=[pl.BlockSpec(memory_space=pltpu.HBM)] * 7,
        out_specs=(any_spec,) * 3,
        scratch_shapes=[
            V((n_dev, cb + width, width_in), bf16),
            V((samples, width_in), bf16),
            V((width, samples), bf16),
            V((s_rows, width_in), bf16),
            V((rank, s_rows), bf16),
            V((1, rank), f32),
            V((width_in, samples), bf16),
            V((1, samples), f32),
            V((s_rows, samples), bf16),
            V((n_dev, cb, samples), bf16),
            V((samples, width), bf16),
            V((rank, samples), f32),
            V((hr, samples), f32),
            V((n_hi, hr, samples), bf16),
            V((width, samples), f32),
            V((hw, samples), f32),
            V((pred_parts, n_hi, hw, samples // pred_parts), bf16),
            V((width, samples), f32),
            V((others, width, cb), bf16),
            V((others, width, cb), bf16),
            V((n_dev, qr, 2 * width), bf16),
            V((2, qr, 2 * width), f32),
            V((width, cb), f32),
            V((width, s_rows), f32),
            dma((7,)), dma((3,)),
            dma((half, ring_parts)), dma((half, ring_parts)), dma((half, ring_parts)), dma((half, ring_parts)),
            dma((4,)), dma((4,)),
            dma((pred_parts,)), dma((pred_parts,)), dma((pred_parts,)), dma((pred_parts,)),
            dma((peers,)), dma((peers,)), dma((pred_parts, peers)), dma((pred_parts, peers)),
            dma((others,)), dma((others,)), dma((others,)), dma((others,)),
        ],
        compiler_params=pltpu.CompilerParams(
            collective_id=0, has_side_effects=True, vmem_limit_bytes=60000 * 1024
        ),
        name="eigenpro_step",
    )(centers, center_weights.T, batch, labels.T, sub_centers, eig_vectors.T, eig_scale.reshape(1, -1))
    outs = pl.pallas_call(
        place,
        out_shape=tuple(jax.ShapeDtypeStruct(out.shape, out.dtype) for out in outs),
        in_specs=[any_spec] * 3,
        out_specs=(any_spec,) * 3,
        scratch_shapes=[dma((3,))],
        name="place_outputs",
    )(*(pltpu.with_memory_space_constraint(out, pltpu.VMEM) for out in outs))
    return tuple(out.T for out in outs)


def solution(mesh):
    placed = (
        P(("grp", "dev"), None),
        P(("grp", "dev"), None),
        P("dev", None),
        P("dev", None),
        P("grp", None),
        P("grp", None),
        P(),
    )
    return jax.shard_map(
        functools.partial(body, mesh.shape["dev"], mesh.shape["grp"]),
        mesh=mesh,
        in_specs=placed,
        out_specs=(P("dev", None), P(("grp", "dev"), None), P("grp", None)),
        check_vma=False,
    )
```
